32 devices in a mesh: groups: 2 (over x), tok: 16 (over z, y, core).
Axes of the slice: x: 2, y: 2, z: 4, core: 2. Of those that a mesh axis runs over, the one named last changes fastest.
Arguments:
- tokens: bfloat16 [4, 8192, 512], P('groups', 'tok'), parts along dimension 0, may hold values from -28 to 28
- w_query: bfloat16 [512, 512], replicated, may hold values from -0.25 to 0.25
- w_key: bfloat16 [512, 512], replicated, may hold values from -0.25 to 0.25
- w_value: bfloat16 [512, 512], replicated, may hold values from -0.25 to 0.25
- w_out: bfloat16 [512, 512], replicated, may hold values from -0.25 to 0.25
- partner_block: int32 [16, 4], P('tok'), may hold values from 0 to 3
- head_masks: int32 [16, 4, 8], P('tok'), may hold values 0 or 1
- cotangent: bfloat16 [4, 8192, 512], P('groups', 'tok'), parts along dimension 0, may hold values from -6 to 6
Outputs:
- output: bfloat16 [4, 8192, 512], P('groups', 'tok'), parts along dimension 0
- grad_tokens: bfloat16 [4, 8192, 512], P('groups', 'tok'), parts along dimension 0
- grad_query: float32 [1024, 512], P('groups'), parts along dimension 0
- grad_key: float32 [1024, 512], P('groups'), parts along dimension 0
- grad_value: float32 [1024, 512], P('groups'), parts along dimension 0
- grad_out: float32 [1024, 512], P('groups'), parts along dimension 0
The draws below stay inside these ranges and needn't reach their ends.
There are 2 independent parts, one for each index of `groups`. The reference program is written for one: setup_inputs(seed, part) draws one part's arguments, and reference() takes and returns one part's arrays. A program takes and returns all parts, laid end to end along the dimension named above; an argument that names none is the same for every part. Nothing has to cross between parts.
All inputs are finite; a program needn't handle non-finite values. No bound on the sum of `head_masks` on one device may be relied on, other than what follows from the above.
Results may differ from the reference program's by a relative error of at most 0.015.
The reference program's roundings to bfloat16 on the way count: a program that leaves them out, or rounds other values in their place, can miss the bound.
Values may be sent and summed in bfloat16 or wider, within the bound.
A program may use at most 128 MiB of HBM per device.

```python
import math
import jax
import jax.numpy as jnp
from jax import lax

SAMPLES = 2
BLOCK = 512
SUB = 128
D = 512
HEADS = 8
HDIM = 64
TOKENS = 8192
N_TOK = 16


def draw_tokens(key, part):
    shape = (SAMPLES, TOKENS, D)
    return jnp.clip(jax.random.normal(key, shape, jnp.float32), -4.0, 4.0).astype(jnp.bfloat16)


def touch_ends(values, key, smallest, top_value):
    index_at = [jax.random.randint(jax.random.fold_in(key, axis), (), 0, length) for axis, length in enumerate(values.shape)]
    longest = values.shape.index(max(values.shape))
    next_to = index_at[:longest] + [(index_at[longest] + 1) % values.shape[longest]] + index_at[longest + 1:]
    return values.at[tuple(index_at)].set(smallest).at[tuple(next_to)].set(top_value)


def block_levels(own_key, shape, cuts, low, high):
    def one(dim, blocks):
        heights = jax.random.uniform(jax.random.fold_in(jax.random.fold_in(own_key, 6), dim), (blocks,), jnp.float32, low / len(cuts), high / len(cuts))
        return jnp.repeat(jnp.exp(heights), shape[dim] // blocks).reshape((-1,) + (1,) * (len(shape) - dim - 1))

    factor_of = one(*cuts[0])
    for cut in cuts[1:]:
        factor_of = factor_of * one(*cut)
    return factor_of


def noise(key, dims, spread, reach, cuts=(), kind=jnp.bfloat16):
    array = jax.random.normal(key, dims, jnp.float32) * spread
    if len(cuts) > 0:
        array = block_levels(key, dims, cuts, -0.22, 0.18) * array
    return jnp.clip(array, min=-reach, max=reach).astype(kind)


def setup_inputs(seed: int = 0, part: int = 0) -> dict:
    key_list = jax.random.split(jax.random.key(seed), 9)
    part_keys = jax.random.split(jax.random.fold_in(key_list[8], part), 9)
    tokens = draw_tokens(jax.random.fold_in(jax.random.fold_in(key_list[8], part), 71), part)
    w_query = noise(key_list[1], (D, D), D ** -0.5, 0.25)
    w_key = noise(key_list[2], (D, D), D ** -0.5, 0.25)
    w_value = noise(key_list[3], (D, D), D ** -0.5, 0.25)
    w_out = noise(key_list[4], (D, D), D ** -0.5, 0.25)
    partner_block = touch_ends(jax.random.randint(key_list[5], (N_TOK, 4), 0, BLOCK // SUB), jax.random.fold_in(key_list[5], 1), 0, (BLOCK // SUB) - 1).astype(jnp.int32)
    head_masks = touch_ends((jax.random.randint(key_list[6], (N_TOK, 4, HEADS), 0, 4) < 3).astype(jnp.int32), jax.random.fold_in(key_list[6], 1), 0, 1)
    cotangent = noise(part_keys[7], (SAMPLES, TOKENS, D), 1.0, 6.0, ((1, 16),))
    return dict(tokens=tokens, w_query=w_query, w_key=w_key, w_value=w_value, w_out=w_out, partner_block=partner_block, head_masks=head_masks, cotangent=cotangent)


def attend(queries, gathered, mask_rows, grad_output, w_out, score_scale):
    samples, block_rows, model_width = queries.shape
    head_count = mask_rows.shape[1]
    head_width = model_width // head_count
    key_count = gathered.shape[1]
    sub_rows = (key_count - block_rows) // 4
    f32 = jnp.float32
    query_heads = queries.reshape(samples, block_rows, head_count, head_width).astype(f32)
    key_heads = gathered[..., :model_width].reshape(samples, key_count, head_count, head_width).astype(f32)
    value_heads = gathered[..., model_width:].reshape(samples, key_count, head_count, head_width).astype(f32)
    visible = jnp.concatenate([jnp.ones((head_count, block_rows), jnp.int32), jnp.repeat(mask_rows.T, sub_rows, axis=1)], 1) > 0
    scores = jnp.einsum('sqhd,skhd->shqk', query_heads, key_heads) * score_scale
    scores = jnp.where(visible[None, :, None, :], scores, -jnp.inf)
    row_max = lax.optimization_barrier(jnp.max(scores, axis=-1, keepdims=True))
    expo_terms = jnp.exp(scores - row_max)
    probability = expo_terms / lax.optimization_barrier(jnp.sum(expo_terms, axis=-1, keepdims=True))
    prob_half = probability.astype(jnp.bfloat16)
    context = jnp.einsum('shqk,skhd->sqhd', prob_half.astype(f32), value_heads).astype(jnp.bfloat16)
    context_rows = context.reshape(samples * block_rows, model_width)
    output = jnp.dot(context_rows, w_out, preferred_element_type=f32).astype(jnp.bfloat16)
    grad_rows = grad_output.reshape(samples * block_rows, model_width)
    grad_context = jnp.dot(grad_rows, w_out.T, preferred_element_type=f32).astype(jnp.bfloat16)
    grad_context = grad_context.reshape(samples, block_rows, head_count, head_width)
    grad_prob = jnp.einsum('sqhd,skhd->shqk', grad_context.astype(f32), value_heads)
    row_dot = lax.optimization_barrier(jnp.sum(grad_context.astype(f32) * context.astype(f32), axis=-1)).transpose(0, 2, 1)
    grad_score = (probability * (grad_prob - row_dot[..., None]) * score_scale).astype(jnp.bfloat16)
    grad_q = jnp.einsum('shqk,skhd->sqhd', grad_score.astype(f32), key_heads).astype(jnp.bfloat16)
    grad_k = jnp.einsum('shqk,sqhd->skhd', grad_score.astype(f32), query_heads)
    grad_v = jnp.einsum('shqk,sqhd->skhd', prob_half.astype(f32), grad_context.astype(f32))
    key_grads = jnp.concatenate([grad_k.reshape(samples, key_count, model_width), grad_v.reshape(samples, key_count, model_width)], -1)
    return (output.reshape(samples, block_rows, model_width), context_rows.reshape(samples, block_rows, model_width), grad_q.reshape(samples, block_rows, model_width), key_grads)

def reference(tokens, w_query, w_key, w_value, w_out, partner_block, head_masks, cotangent):
    f32 = jnp.float32
    score_scale = 1.0 / math.sqrt(HDIM)
    levels = N_TOK.bit_length() - 1
    token_rows = tokens.reshape(SAMPLES * TOKENS, D)
    queries = jnp.dot(token_rows, w_query, preferred_element_type=f32).astype(jnp.bfloat16).reshape(SAMPLES, TOKENS, D)
    w_key_value = jnp.concatenate([w_key, w_value], 1)
    key_value = jnp.dot(token_rows, w_key_value, preferred_element_type=f32).astype(jnp.bfloat16).reshape(SAMPLES, TOKENS, 2 * D)

    def one_block(key_grads, block_index):
        first_row = (block_index * BLOCK).astype(jnp.int32)
        window_queries = lax.dynamic_slice_in_dim(queries, first_row, BLOCK, 1)
        pieces = [lax.dynamic_slice_in_dim(key_value, first_row, BLOCK, 1)]
        starts = [first_row]
        for section in range(4):
            partner_dev = jnp.bitwise_xor(block_index, 1 << levels - 4 + section)
            start_row = (partner_dev * BLOCK + partner_block[block_index, section] * SUB).astype(jnp.int32)
            pieces.append(lax.dynamic_slice_in_dim(key_value, start_row, SUB, 1))
            starts.append(start_row)
        gathered = jnp.concatenate(pieces, 1)
        grad_output = lax.dynamic_slice_in_dim(cotangent, first_row, BLOCK, 1)
        output, context, grad_q, block_grads = attend(window_queries, gathered, head_masks[block_index], grad_output, w_out, score_scale)
        offset = 0
        for start_row, row_count in zip(starts, [BLOCK, SUB, SUB, SUB, SUB]):
            addend = block_grads[:, offset:offset + row_count]
            current = lax.dynamic_slice_in_dim(key_grads, start_row, row_count, 1)
            key_grads = lax.dynamic_update_slice_in_dim(key_grads, current + addend, start_row, 1)
            offset += row_count
        return (key_grads, (output, context, grad_q))
    initial = jnp.zeros((SAMPLES, TOKENS, 2 * D), f32)
    key_grads, (outputs, contexts, grad_qs) = lax.scan(one_block, initial, jnp.arange(N_TOK, dtype=jnp.int32))

    def merge_blocks(stacked):
        return stacked.transpose(1, 0, 2, 3).reshape(SAMPLES * TOKENS, D)
    output = merge_blocks(outputs).reshape(SAMPLES, TOKENS, D)
    context_rows = merge_blocks(contexts)
    grad_q_rows = merge_blocks(grad_qs)
    grad_kv_rows = key_grads.astype(jnp.bfloat16).reshape(SAMPLES * TOKENS, 2 * D)
    grad_tokens = (jnp.dot(grad_q_rows, w_query.T, preferred_element_type=f32) + jnp.dot(grad_kv_rows, w_key_value.T, preferred_element_type=f32)).astype(jnp.bfloat16)
    grad_query = jnp.dot(token_rows.T, grad_q_rows, preferred_element_type=f32)
    grad_pair = jnp.dot(token_rows.T, grad_kv_rows, preferred_element_type=f32)
    grad_out = jnp.dot(context_rows.T, cotangent.reshape(SAMPLES * TOKENS, D), preferred_element_type=f32)
    return (output, grad_tokens.reshape(SAMPLES, TOKENS, D), grad_query, grad_pair[:, :D], grad_pair[:, D:], grad_out)
```

```python
import functools
import math

import jax
import jax.numpy as jnp
from jax import lax
from jax.experimental import pallas as pl
from jax.experimental.pallas import tpu as pltpu
from jax.sharding import PartitionSpec as P

SUB = 128
SECTIONS = 4
LANES = 128
F32 = jnp.float32
BF16 = jnp.bfloat16


def partner(x, axis, stride):
    return lax.ppermute(x, axis, [(i, i ^ 1 << stride) for i in range(lax.axis_size(axis))])


def nt(a, b):
    return lax.dot_general(a, b, (((1,), (1,)), ((), ())), preferred_element_type=F32)


def mm(a, b):
    return jnp.dot(a, b, preferred_element_type=F32)


def attend_kernel(
    group, head_width, scale,
    mask_ref, tok_ref, arr_ref, cot_ref, wq_ref, wk_ref, wv_ref, wo_ref,
    ctx_ref, dq_ref, own_ref, part_ref, gw_ref, go_ref,
    x_ref, gq_acc, gk_acc, gv_acc, go_acc,
):
    sample = pl.program_id(0)
    rows = tok_ref.shape[1]
    keys = x_ref.shape[0]
    x_ref[:rows, :] = tok_ref[0]
    for s in range(SECTIONS):
        x_ref[rows + s * SUB : rows + (s + 1) * SUB, :] = arr_ref[s, 0]
    tok = tok_ref[0]
    x = x_ref[...]
    cot = cot_ref[0]
    q = (mm(tok, wq_ref[...]).astype(BF16).astype(F32) * scale).astype(BF16)
    k = mm(x, wk_ref[...]).astype(BF16)
    v = mm(x, wv_ref[...]).astype(BF16)
    gc = nt(cot, wo_ref[...]).astype(BF16)
    k_t, v_t, gc_t = k.T, v.T, gc.T
    lane = lax.broadcasted_iota(jnp.int32, (rows, LANES), 1)
    heads = LANES // head_width
    dk = dv = None
    ctx_t, dq_t = [], []
    for h in range(heads):
        here = (lane >= h * head_width) & (lane < (h + 1) * head_width)
        qh = jnp.where(here, q, jnp.zeros_like(q))
        gh = jnp.where(here, gc, jnp.zeros_like(gc))
        span = slice(h * head_width, (h + 1) * head_width)
        scores = nt(k, qh)
        parts = [scores[:rows]]
        for s in range(SECTIONS):
            piece = scores[rows + s * SUB : rows + (s + 1) * SUB]
            on = mask_ref[0, s, group * heads + h] > 0
            parts.append(jnp.where(on, piece, -jnp.inf))
        scores = jnp.concatenate(parts, 0)
        top = jnp.max(scores, axis=0, keepdims=True)
        expo = jnp.exp(scores - top)
        prob = expo * (1.0 / jnp.sum(expo, axis=0, keepdims=True))
        half = prob.astype(BF16)
        c_t = mm(v_t[span], half).astype(BF16)
        grad_prob = nt(v, gh)
        row_dot = jnp.sum(gc_t[span].astype(F32) * c_t.astype(F32), axis=0, keepdims=True)
        ds = (prob * (grad_prob - row_dot)).astype(BF16)
        dq_t.append((mm(k_t[span], ds) * scale).astype(BF16))
        ctx_t.append(c_t)
        dk_h, dv_h = mm(ds, qh), mm(half, gh)
        dk = dk_h if dk is None else dk + dk_h
        dv = dv_h if dv is None else dv + dv_h
    ctx_t = jnp.concatenate(ctx_t, 0)
    dq_t = jnp.concatenate(dq_t, 0)
    ctx_ref[0] = ctx_t.T
    dq_ref[0] = dq_t.T
    own_ref[0, :, :LANES] = dk[:rows]
    own_ref[0, :, LANES:] = dv[:rows]
    dkb, dvb = dk.astype(BF16), dv.astype(BF16)
    for s in range(SECTIONS):
        at = slice(rows + s * SUB, rows + (s + 1) * SUB)
        part_ref[s, 0, :, :LANES] = dkb[at]
        part_ref[s, 0, :, LANES:] = dvb[at]
    terms = (
        (gq_acc, mm(dq_t, tok)),
        (gk_acc, mm(dkb.T, x)),
        (gv_acc, mm(dvb.T, x)),
        (go_acc, mm(ctx_t, cot)),
    )

    @pl.when(sample == 0)
    def _():
        for acc, term in terms:
            acc[...] = term

    @pl.when(sample > 0)
    def _():
        for acc, term in terms:
            acc[...] += term

    @pl.when(sample == pl.num_programs(0) - 1)
    def _():
        for i, acc in enumerate((gq_acc, gk_acc, gv_acc)):
            gw_ref[:, i * LANES : (i + 1) * LANES] = acc[...].T.astype(BF16)
        go_ref[...] = go_acc[...].astype(BF16)


def attend(group, head_width, masks, tokens, arrived, cotangent, w_query, w_key, w_value, w_out):
    samples, rows, width = tokens.shape
    keys = rows + SECTIONS * SUB
    scale = 1.0 / math.sqrt(head_width)
    columns = pl.BlockSpec((width, LANES), lambda i: (0, group))
    flops = samples * (12 * rows * keys * LANES * 2 + 14 * rows * width * LANES)
    return pl.pallas_call(
        functools.partial(attend_kernel, group, head_width, scale),
        grid=(samples,),
        in_specs=[
            pl.BlockSpec(memory_space=pltpu.SMEM),
            pl.BlockSpec((1, rows, width), lambda i: (i, 0, 0)),
            pl.BlockSpec((SECTIONS, 1, SUB, width), lambda i: (0, i, 0, 0)),
            pl.BlockSpec((1, rows, width), lambda i: (i, 0, 0)),
            columns,
            columns,
            columns,
            pl.BlockSpec((LANES, width), lambda i: (group, 0)),
        ],
        out_specs=[
            pl.BlockSpec((1, rows, LANES), lambda i: (i, 0, 0)),
            pl.BlockSpec((1, rows, LANES), lambda i: (i, 0, 0)),
            pl.BlockSpec((1, rows, 2 * LANES), lambda i: (i, 0, 0)),
            pl.BlockSpec((SECTIONS, 1, SUB, 2 * LANES), lambda i: (0, i, 0, 0)),
            pl.BlockSpec((width, 3 * LANES), lambda i: (0, 0)),
            pl.BlockSpec((LANES, width), lambda i: (0, 0)),
        ],
        out_shape=[
            jax.ShapeDtypeStruct((samples, rows, LANES), BF16),
            jax.ShapeDtypeStruct((samples, rows, LANES), BF16),
            jax.ShapeDtypeStruct((samples, rows, 2 * LANES), F32),
            jax.ShapeDtypeStruct((SECTIONS, samples, SUB, 2 * LANES), BF16),
            jax.ShapeDtypeStruct((width, 3 * LANES), BF16),
            jax.ShapeDtypeStruct((LANES, width), BF16),
        ],
        scratch_shapes=[pltpu.VMEM((keys, width), BF16)]
        + [pltpu.VMEM((LANES, width), F32)] * 4,
        cost_estimate=pl.CostEstimate(
            flops=flops, bytes_accessed=8 << 20, transcendentals=samples * rows * keys * 2
        ),
        compiler_params=pltpu.CompilerParams(vmem_limit_bytes=48 << 20),
        name="attend",
    )(masks, tokens, arrived, cotangent, w_query, w_key, w_value, w_out)


def per_device(tokens, w_query, w_key, w_value, w_out, partner_block, head_masks, cotangent):
    samples, rows, width = tokens.shape
    levels = lax.axis_size("tok").bit_length() - 1
    head_width = width // head_masks.shape[2]
    sent_starts, arrived = [], []
    for s in range(SECTIONS):
        theirs = partner(partner_block, "tok", levels - 4 + s)
        sent_starts.append(theirs[0, s] * SUB)
    for s in reversed(range(SECTIONS)):
        chosen = lax.dynamic_slice_in_dim(tokens, sent_starts[s], SUB, 1)
        arrived.append(partner(chosen, "tok", levels - 4 + s))
    arrived = jnp.stack(arrived[::-1], 0)
    contexts, grad_qs, key_grads, summed = [], [], [], []
    for group in range(width // LANES):
        ctx, dq, own, part, gw, go = attend(
            group, head_width, head_masks, tokens, arrived, cotangent, w_query, w_key, w_value, w_out
        )
        contexts.append(ctx)
        grad_qs.append(dq)
        if summed:
            gw, go, _ = lax.optimization_barrier((gw, go, summed[-1]))
        summed.append(lax.psum((gw, go), "tok"))
        for s in reversed(range(SECTIONS)):
            returned = partner(part[s], "tok", levels - 4 + s).astype(F32)
            current = lax.dynamic_slice_in_dim(own, sent_starts[s], SUB, 1)
            own = lax.dynamic_update_slice_in_dim(own, current + returned, sent_starts[s], 1)
        key_grads.append(own.astype(BF16))
    flat = lambda items: jnp.concatenate(items, -1).reshape(samples * rows, -1)
    output = mm(flat(contexts), w_out).astype(BF16).reshape(samples, rows, width)
    grad_kv = key_grads
    dk = flat([g[..., :LANES] for g in grad_kv])
    dv = flat([g[..., LANES:] for g in grad_kv])
    grad_tokens = (nt(flat(grad_qs), w_query) + nt(dk, w_key) + nt(dv, w_value)).astype(BF16)
    weights = [
        jnp.concatenate([s[0][:, i * LANES : (i + 1) * LANES] for s in summed], 1).astype(F32)
        for i in range(3)
    ]
    grad_out = jnp.concatenate([s[1] for s in summed], 0).astype(F32)
    return (output, grad_tokens.reshape(samples, rows, width), *weights, grad_out)


def solution(mesh):
    placed = (
        P("groups", "tok", None),
        P(),
        P(),
        P(),
        P(),
        P("tok", None),
        P("tok", None, None),
        P("groups", "tok", None),
    )
    return jax.shard_map(
        per_device,
        mesh=mesh,
        in_specs=placed,
        out_specs=(
            P("groups", "tok", None),
            P("groups", "tok", None),
            P("groups", None),
            P("groups", None),
            P("groups", None),
            P("groups", None),
        ),
        check_vma=False,
    )
```

```python
import functools
import math

import jax
import jax.numpy as jnp
from jax import lax
from jax.experimental import pallas as pl
from jax.experimental.pallas import tpu as pltpu
from jax.sharding import PartitionSpec as P

SUB = 128
SECTIONS = 4
LANES = 128
F32 = jnp.float32
BF16 = jnp.bfloat16
MESH = pl.DeviceIdType.MESH


def nt(a, b):
    return lax.dot_general(a, b, (((1,), (1,)), ((), ())), preferred_element_type=F32)


def mm(a, b):
    return jnp.dot(a, b, preferred_element_type=F32)


def attend_kernel(
    head_width, scale,
    mask_ref, tok_ref, arr_ref, cot_ref, wq_ref, wk_ref, wv_ref, wo_ref,
    ctx_ref, dq_ref, own_ref, part_ref, gw_ref, go_ref,
    x_ref, gq_acc, gk_acc, gv_acc, go_acc,
):
    group, sample = pl.program_id(0), pl.program_id(1)
    rows = tok_ref.shape[1]
    keys = x_ref.shape[0]
    x_ref[:rows, :] = tok_ref[0]
    for s in range(SECTIONS):
        x_ref[rows + s * SUB : rows + (s + 1) * SUB, :] = arr_ref[s, 0]
    tok = tok_ref[0]
    x = x_ref[...]
    cot = cot_ref[0]
    q = (mm(tok, wq_ref[...]).astype(BF16).astype(F32) * scale).astype(BF16)
    k = mm(x, wk_ref[...]).astype(BF16)
    v = mm(x, wv_ref[...]).astype(BF16)
    gc = nt(cot, wo_ref[...]).astype(BF16)
    k_t, v_t, gc_t = k.T, v.T, gc.T
    lane = lax.broadcasted_iota(jnp.int32, (rows, LANES), 1)
    heads = LANES // head_width
    dk = dv = None
    ctx_t, dq_t = [], []
    for h in range(heads):
        here = (lane >= h * head_width) & (lane < (h + 1) * head_width)
        qh = jnp.where(here, q, jnp.zeros_like(q))
        gh = jnp.where(here, gc, jnp.zeros_like(gc))
        span = slice(h * head_width, (h + 1) * head_width)
        scores = nt(k, qh)
        parts = [scores[:rows]]
        for s in range(SECTIONS):
            piece = scores[rows + s * SUB : rows + (s + 1) * SUB]
            on = mask_ref[0, s, group * heads + h] > 0
            parts.append(jnp.where(on, piece, -jnp.inf))
        scores = jnp.concatenate(parts, 0)
        top = jnp.max(scores, axis=0, keepdims=True)
        expo = jnp.exp(scores - top)
        prob = expo * (1.0 / jnp.sum(expo, axis=0, keepdims=True))
        half = prob.astype(BF16)
        c_t = mm(v_t[span], half).astype(BF16)
        grad_prob = nt(v, gh)
        row_dot = jnp.sum(gc_t[span].astype(F32) * c_t.astype(F32), axis=0, keepdims=True)
        ds = (prob * (grad_prob - row_dot)).astype(BF16)
        dq_t.append((mm(k_t[span], ds) * scale).astype(BF16))
        ctx_t.append(c_t)
        dk_h, dv_h = mm(ds, qh), mm(half, gh)
        dk = dk_h if dk is None else dk + dk_h
        dv = dv_h if dv is None else dv + dv_h
    ctx_t = jnp.concatenate(ctx_t, 0)
    dq_t = jnp.concatenate(dq_t, 0)
    ctx_ref[0] = ctx_t.T
    dq_ref[0] = dq_t.T
    own_ref[0, 0] = dk[:rows]
    own_ref[1, 0] = dv[:rows]
    dkb, dvb = dk.astype(BF16), dv.astype(BF16)
    for s in range(SECTIONS):
        at = slice(rows + s * SUB, rows + (s + 1) * SUB)
        part_ref[s, 0, 0] = dkb[at]
        part_ref[s, 1, 0] = dvb[at]
    terms = (
        (gq_acc, mm(dq_t, tok)),
        (gk_acc, mm(dkb.T, x)),
        (gv_acc, mm(dvb.T, x)),
        (go_acc, mm(ctx_t, cot)),
    )

    @pl.when(sample == 0)
    def _():
        for acc, term in terms:
            acc[...] = term

    @pl.when(sample > 0)
    def _():
        for acc, term in terms:
            acc[...] += term

    @pl.when(sample == pl.num_programs(1) - 1)
    def _():
        for i, acc in enumerate((gq_acc, gk_acc, gv_acc)):
            gw_ref[i] = acc[...].T.astype(BF16)
        go_ref[...] = go_acc[...].astype(BF16)


def attend(head_width, masks, tokens, arrived, cotangent, w_query, w_key, w_value, w_out):
    samples, rows, width = tokens.shape
    keys = rows + SECTIONS * SUB
    scale = 1.0 / math.sqrt(head_width)
    columns = pl.BlockSpec((width, LANES), lambda g, i: (0, g))
    whole_row = pl.BlockSpec((1, rows, width), lambda g, i: (i, 0, 0))
    row_columns = pl.BlockSpec((1, rows, LANES), lambda g, i: (i, 0, g))
    return pl.pallas_call(
        functools.partial(attend_kernel, head_width, scale),
        grid=(width // LANES, samples),
        in_specs=[
            pl.BlockSpec(memory_space=pltpu.SMEM),
            whole_row,
            pl.BlockSpec((SECTIONS, 1, SUB, width), lambda g, i: (0, i, 0, 0)),
            whole_row,
            columns,
            columns,
            columns,
            pl.BlockSpec((LANES, width), lambda g, i: (g, 0)),
        ],
        out_specs=[
            row_columns,
            row_columns,
            pl.BlockSpec((2, 1, rows, LANES), lambda g, i: (0, i, 0, g)),
            pl.BlockSpec((SECTIONS, 2, 1, SUB, LANES), lambda g, i: (0, 0, i, 0, g)),
            pl.BlockSpec((3, width, LANES), lambda g, i: (0, 0, g)),
            pl.BlockSpec((LANES, width), lambda g, i: (g, 0)),
        ],
        out_shape=[
            jax.ShapeDtypeStruct((samples, rows, width), BF16),
            jax.ShapeDtypeStruct((samples, rows, width), BF16),
            jax.ShapeDtypeStruct((2, samples, rows, width), F32),
            jax.ShapeDtypeStruct((SECTIONS, 2, samples, SUB, width), BF16),
            jax.ShapeDtypeStruct((3, width, width), BF16),
            jax.ShapeDtypeStruct((width, width), BF16),
        ],
        scratch_shapes=[pltpu.VMEM((keys, width), BF16)]
        + [pltpu.VMEM((LANES, width), F32)] * 4,
        compiler_params=pltpu.CompilerParams(vmem_limit_bytes=48 << 20),
        name="attend",
    )(masks, tokens, arrived, cotangent, w_query, w_key, w_value, w_out)


def toward(bit):
    me = lax.axis_index("tok")
    mine = (me // (1 << bit)) % 2
    return mine, {"tok": me + (1 - 2 * mine) * (1 << bit)}


def greet(bits):
    barrier = pltpu.get_barrier_semaphore()
    for bit in bits:
        pl.semaphore_signal(barrier, inc=1, device_id=toward(bit)[1], device_id_type=MESH)
    pl.semaphore_wait(barrier, len(bits))


def send(src, dst, send_sem, recv_sem, bit):
    copy = pltpu.make_async_remote_copy(
        src_ref=src, dst_ref=dst, send_sem=send_sem, recv_sem=recv_sem,
        device_id=toward(bit)[1], device_id_type=MESH,
    )
    copy.start()
    return copy


def fetch_kernel(
    levels, choice_ref, tok_ref, arrived_ref, theirs_ref,
    chosen, landed, wanted, choice_send, choice_recv, tok_send, tok_recv,
):
    samples, rows, width = tok_ref.shape
    first = levels - SECTIONS
    greet([first + s for s in range(SECTIONS)])
    asks = [
        send(choice_ref.at[s], wanted.at[s], choice_send.at[s], choice_recv.at[s], first + s)
        for s in range(SECTIONS)
    ]
    copies = []
    for s in reversed(range(SECTIONS)):
        asks[s].wait()
        pick = jnp.broadcast_to(wanted[s, 0:1, 0:1], (SUB, width))
        for i in range(samples):
            value = tok_ref[i, :SUB, :].astype(F32)
            for block in range(1, rows // SUB):
                other = tok_ref[i, block * SUB : (block + 1) * SUB, :].astype(F32)
                value = jnp.where(pick == block, other, value)
            chosen[s, i] = value.astype(BF16)
        copies.append(
            (s, send(chosen.at[s], landed.at[s], tok_send.at[s], tok_recv.at[s], first + s))
        )
    theirs_ref[...] = wanted[...]
    for s, copy in reversed(copies):
        copy.wait()
        arrived_ref[s] = landed[s]


def fetch(levels, choice, tokens):
    samples, rows, width = tokens.shape
    vmem = pl.BlockSpec(memory_space=pltpu.VMEM)
    size = (SECTIONS, samples, SUB, width)
    sems = pltpu.SemaphoreType.DMA((SECTIONS,))
    return pl.pallas_call(
        functools.partial(fetch_kernel, levels),
        in_specs=[vmem, vmem],
        out_specs=[vmem, vmem],
        out_shape=[
            jax.ShapeDtypeStruct(size, BF16),
            jax.ShapeDtypeStruct(choice.shape, jnp.int32),
        ],
        scratch_shapes=[
            pltpu.VMEM(size, BF16),
            pltpu.VMEM(size, BF16),
            pltpu.VMEM(choice.shape, jnp.int32),
            sems, sems, sems, sems,
        ],
        compiler_params=pltpu.CompilerParams(collective_id=0, has_side_effects=True),
        name="fetch",
    )(choice, tokens)


def settle_kernel(
    levels, part_ref, gw_ref, go_ref, ret_ref, sum_ref,
    landed, acc, got, full, part_send, part_recv, rs_send, rs_recv, ag_send, ag_recv,
):
    width = go_ref.shape[0]
    for i in range(3):
        acc[i * width : (i + 1) * width, :] = gw_ref[i]
    acc[3 * width :, :] = go_ref[...]
    greet(list(range(levels)))
    half_rows = 2 * width
    straight = list(range(levels))
    orders = (straight, [0] + straight[2:] + [1])
    base = [lane * half_rows for lane in range(2)]
    size, inbox = half_rows, [lane * half_rows for lane in range(2)]
    lanes = range(2)

    def window(ref, start, count):
        return ref.at[pl.ds(pl.multiple_of(start, count), count), :]

    def scatter(lane, step, size):
        bit, half = orders[lane][step], size // 2
        mine, _ = toward(bit)
        away = base[lane] + (1 - mine) * half
        copy = send(
            window(acc, away, half), window(got, inbox[lane], half),
            rs_send.at[lane, step], rs_recv.at[lane, step], bit,
        )
        base[lane] = base[lane] + mine * half
        return copy

    flying = [scatter(lane, 0, size) for lane in lanes]
    first = levels - SECTIONS
    returns = [
        send(part_ref.at[s], landed.at[s], part_send.at[s], part_recv.at[s], first + s)
        for s in reversed(range(SECTIONS))
    ]
    for step in range(levels):
        half = size // 2
        for lane in lanes:
            flying[lane].wait()
            here = pl.ds(pl.multiple_of(base[lane], half), half)
            total = acc[here, :].astype(F32) + got[inbox[lane] : inbox[lane] + half, :].astype(F32)
            inbox[lane] += half
            if step < levels - 1:
                acc[here, :] = total.astype(BF16)
                flying[lane] = scatter(lane, step + 1, half)
            else:
                full[here, :] = total.astype(BF16)
        size = half
    for step in reversed(range(levels)):
        for lane in lanes:
            if step < levels - 1:
                flying[lane].wait()
                base[lane] = base[lane] - toward(orders[lane][step + 1])[0] * (size // 2)
            held = window(full, base[lane], size)
            flying[lane] = send(
                held, held, ag_send.at[lane, step], ag_recv.at[lane, step], orders[lane][step]
            )
        size *= 2
    for lane in lanes:
        flying[lane].wait()
    sum_ref[...] = full[...]
    for copy in returns:
        copy.wait()
    ret_ref[...] = landed[...]


def settle(levels, part, gw, go):
    width = go.shape[0]
    vmem = pl.BlockSpec(memory_space=pltpu.VMEM)
    stack = (4 * width, width)
    four = pltpu.SemaphoreType.DMA((SECTIONS,))
    steps = pltpu.SemaphoreType.DMA((2, levels))
    return pl.pallas_call(
        functools.partial(settle_kernel, levels),
        in_specs=[vmem] * 3,
        out_specs=[vmem] * 2,
        out_shape=[
            jax.ShapeDtypeStruct(part.shape, BF16),
            jax.ShapeDtypeStruct(stack, BF16),
        ],
        scratch_shapes=[pltpu.VMEM(part.shape, BF16)]
        + [pltpu.VMEM(stack, BF16)] * 3
        + [four, four, steps, steps, steps, steps],
        compiler_params=pltpu.CompilerParams(
            collective_id=1, has_side_effects=True, vmem_limit_bytes=48 << 20
        ),
        name="settle",
    )(part, gw, go)


def finish_kernel(
    start_ref, own_ref, ret_ref, ctx_ref, dq_ref, wq_ref, wk_ref, wv_ref, wo_ref, sum_ref,
    out_ref, gtok_ref, gq_ref, gk_ref, gv_ref, go_ref, key_grads,
):
    out_ref[0] = mm(ctx_ref[0], wo_ref[...]).astype(BF16)
    key_grads[...] = own_ref[:, 0]
    for s in range(SECTIONS):
        at = pl.ds(pl.multiple_of(start_ref[s], SUB), SUB)
        key_grads[:, at, :] += ret_ref[s, :, 0].astype(F32)
    gtok_ref[0] = (
        nt(dq_ref[0], wq_ref[...])
        + nt(key_grads[0].astype(BF16), wk_ref[...])
        + nt(key_grads[1].astype(BF16), wv_ref[...])
    ).astype(BF16)
    for i, ref in enumerate((gq_ref, gk_ref, gv_ref, go_ref)):
        ref[...] = sum_ref[i].astype(F32)


def finish(starts, own, ret, ctx, dq, w_query, w_key, w_value, w_out, sums):
    samples, rows, width = ctx.shape
    row = pl.BlockSpec((1, rows, width), lambda i: (i, 0, 0))
    weight = pl.BlockSpec((width, width), lambda i: (0, 0))
    share = width // samples
    grad = pl.BlockSpec((share, width), lambda i: (i, 0))
    return pl.pallas_call(
        finish_kernel,
        grid=(samples,),
        in_specs=[
            pl.BlockSpec(memory_space=pltpu.SMEM),
            pl.BlockSpec((2, 1, rows, width), lambda i: (0, i, 0, 0)),
            pl.BlockSpec((SECTIONS, 2, 1, SUB, width), lambda i: (0, 0, i, 0, 0)),
            row, row, weight, weight, weight, weight,
            pl.BlockSpec((4, share, width), lambda i: (0, i, 0)),
        ],
        out_specs=[row, row, grad, grad, grad, grad],
        out_shape=[jax.ShapeDtypeStruct(ctx.shape, BF16)] * 2
        + [jax.ShapeDtypeStruct((width, width), F32)] * 4,
        scratch_shapes=[pltpu.VMEM((2, rows, width), F32)],
        compiler_params=pltpu.CompilerParams(vmem_limit_bytes=48 << 20),
        name="finish",
    )(starts, own, ret, ctx, dq, w_query, w_key, w_value, w_out, sums)


def per_device(tokens, w_query, w_key, w_value, w_out, partner_block, head_masks, cotangent):
    width = tokens.shape[2]
    levels = lax.axis_size("tok").bit_length() - 1
    head_width = width // head_masks.shape[2]
    choice = jnp.broadcast_to(partner_block[0][:, None, None], (SECTIONS, 8, LANES))
    arrived, theirs = fetch(levels, choice, tokens)
    ctx, dq, own, part, gw, go = attend(
        head_width, head_masks, tokens, arrived, cotangent, w_query, w_key, w_value, w_out
    )
    ret, sums = settle(levels, part, gw, go)
    starts = theirs[:, 0, 0] * SUB
    return finish(
        starts, own, ret, ctx, dq, w_query, w_key, w_value, w_out, sums.reshape(4, width, width)
    )


def solution(mesh):
    placed = (
        P("groups", "tok", None),
        P(),
        P(),
        P(),
        P(),
        P("tok", None),
        P("tok", None, None),
        P("groups", "tok", None),
    )
    return jax.shard_map(
        per_device,
        mesh=mesh,
        in_specs=placed,
        out_specs=(
            P("groups", "tok", None),
            P("groups", "tok", None),
            P("groups", None),
            P("groups", None),
            P("groups", None),
            P("groups", None),
        ),
        check_vma=False,
    )
```

```python
import functools
import math

import jax
import jax.numpy as jnp
from jax import lax
from jax.experimental import pallas as pl
from jax.experimental.pallas import tpu as pltpu
from jax.sharding import PartitionSpec as P


SUB = 128
SECTIONS = 4
LANES = 128
LATE = 1
F32 = jnp.float32
BF16 = jnp.bfloat16
MESH = pl.DeviceIdType.MESH


def partner(x, axis, stride):
    return lax.ppermute(x, axis, [(i, i ^ 1 << stride) for i in range(lax.axis_size(axis))])


def nt(a, b):
    return lax.dot_general(a, b, (((1,), (1,)), ((), ())), preferred_element_type=F32)


def mm(a, b):
    return jnp.dot(a, b, preferred_element_type=F32)


def attend_kernel(
    head_width, scale, first, held,
    mask_ref, tok_ref, arr_ref, cot_ref, wq_ref, wk_ref, wv_ref, wo_ref, *refs,
):
    ctx_ref, dq_ref, own_ref, gw_ref, go_ref, part_ref = refs[held : held + 6]
    x_ref, gq_acc, gk_acc, gv_acc, go_acc = refs[held + 6 :]
    group, sample = first + pl.program_id(0), pl.program_id(1)
    rows = tok_ref.shape[1]
    x_ref[:rows, :] = tok_ref[0]
    for s in range(SECTIONS):
        x_ref[rows + s * SUB : rows + (s + 1) * SUB, :] = arr_ref[s, 0]
    tok = tok_ref[0]
    x = x_ref[...]
    cot = cot_ref[0]
    q = (mm(tok, wq_ref[...]).astype(BF16).astype(F32) * scale).astype(BF16)
    k = mm(x, wk_ref[...]).astype(BF16)
    v = mm(x, wv_ref[...]).astype(BF16)
    gc = nt(cot, wo_ref[...]).astype(BF16)
    k_t, v_t, gc_t = k.T, v.T, gc.T
    lane = lax.broadcasted_iota(jnp.int32, (rows, LANES), 1)
    heads = LANES // head_width
    dk = dv = None
    ctx_t, dq_t = [], []
    for h in range(heads):
        here = (lane >= h * head_width) & (lane < (h + 1) * head_width)
        qh = jnp.where(here, q, jnp.zeros_like(q))
        gh = jnp.where(here, gc, jnp.zeros_like(gc))
        span = slice(h * head_width, (h + 1) * head_width)
        scores = nt(k, qh)
        parts = [scores[:rows]]
        for s in range(SECTIONS):
            piece = scores[rows + s * SUB : rows + (s + 1) * SUB]
            on = mask_ref[0, s, group * heads + h] > 0
            parts.append(jnp.where(on, piece, -jnp.inf))
        scores = jnp.concatenate(parts, 0)
        top = jnp.max(scores, axis=0, keepdims=True)
        expo = jnp.exp(scores - top)
        prob = expo * (1.0 / jnp.sum(expo, axis=0, keepdims=True))
        half = prob.astype(BF16)
        c_t = mm(v_t[span], half).astype(BF16)
        grad_prob = nt(v, gh)
        row_dot = jnp.sum(gc_t[span].astype(F32) * c_t.astype(F32), axis=0, keepdims=True)
        ds = (prob * (grad_prob - row_dot)).astype(BF16)
        dq_t.append((mm(k_t[span], ds) * scale).astype(BF16))
        ctx_t.append(c_t)
        dk_h, dv_h = mm(ds, qh), mm(half, gh)
        dk = dk_h if dk is None else dk + dk_h
        dv = dv_h if dv is None else dv + dv_h
    ctx_t = jnp.concatenate(ctx_t, 0)
    dq_t = jnp.concatenate(dq_t, 0)
    ctx_ref[0] = ctx_t.T
    dq_ref[0] = dq_t.T
    own_ref[0, 0] = dk[:rows]
    own_ref[1, 0] = dv[:rows]
    dkb, dvb = dk.astype(BF16), dv.astype(BF16)
    for s in range(SECTIONS):
        at = slice(rows + s * SUB, rows + (s + 1) * SUB)
        part_ref[s, 0, 0] = dkb[at]
        part_ref[s, 1, 0] = dvb[at]
    terms = (
        (gq_acc, mm(dq_t, tok)),
        (gk_acc, mm(dkb.T, x)),
        (gv_acc, mm(dvb.T, x)),
        (go_acc, mm(ctx_t, cot)),
    )

    @pl.when(sample == 0)
    def _():
        for acc, term in terms:
            acc[...] = term

    @pl.when(sample > 0)
    def _():
        for acc, term in terms:
            acc[...] += term

    @pl.when(sample == pl.num_programs(1) - 1)
    def _():
        for i, acc in enumerate((gq_acc, gk_acc, gv_acc)):
            gw_ref[i] = acc[...].T.astype(BF16)
        go_ref[...] = go_acc[...].astype(BF16)


def attend(
    head_width, first, count, held,
    masks, tokens, arrived, cotangent, w_query, w_key, w_value, w_out,
):
    samples, rows, width = tokens.shape
    keys = rows + SECTIONS * SUB
    scale = 1.0 / math.sqrt(head_width)
    columns = pl.BlockSpec((width, LANES), lambda g, i: (0, first + g))
    whole_row = pl.BlockSpec((1, rows, width), lambda g, i: (i, 0, 0))
    row_columns = pl.BlockSpec((1, rows, LANES), lambda g, i: (i, 0, first + g))
    return pl.pallas_call(
        functools.partial(attend_kernel, head_width, scale, first, len(held)),
        grid=(count, samples),
        in_specs=[
            pl.BlockSpec(memory_space=pltpu.SMEM),
            whole_row,
            pl.BlockSpec((SECTIONS, 1, SUB, width), lambda g, i: (0, i, 0, 0)),
            whole_row,
            columns,
            columns,
            columns,
            pl.BlockSpec((LANES, width), lambda g, i: (first + g, 0)),
        ]
        + [pl.BlockSpec(memory_space=pl.ANY)] * len(held),
        out_specs=[
            row_columns,
            row_columns,
            pl.BlockSpec((2, 1, rows, LANES), lambda g, i: (0, i, 0, first + g)),
            pl.BlockSpec((3, width, LANES), lambda g, i: (0, 0, first + g)),
            pl.BlockSpec((LANES, width), lambda g, i: (first + g, 0)),
            pl.BlockSpec((SECTIONS, 2, 1, SUB, LANES), lambda g, i: (0, 0, i, 0, g)),
        ],
        out_shape=[
            jax.ShapeDtypeStruct((samples, rows, width), BF16),
            jax.ShapeDtypeStruct((samples, rows, width), BF16),
            jax.ShapeDtypeStruct((2, samples, rows, width), F32),
            jax.ShapeDtypeStruct((3, width, width), BF16),
            jax.ShapeDtypeStruct((width, width), BF16),
            jax.ShapeDtypeStruct((SECTIONS, 2, samples, SUB, count * LANES), BF16),
        ],
        input_output_aliases={8 + i: i for i in range(len(held))},
        scratch_shapes=[pltpu.VMEM((keys, width), BF16)]
        + [pltpu.VMEM((LANES, width), F32)] * 4,
        cost_estimate=pl.CostEstimate(
            flops=count * samples * (24 * rows * keys * LANES + 14 * rows * width * LANES),
            bytes_accessed=16 << 20,
            transcendentals=count * samples * rows * keys * 2,
        ),
        name="attend",
    )(masks, tokens, arrived, cotangent, w_query, w_key, w_value, w_out, *held)


def toward(bit):
    me = lax.axis_index("tok")
    mine = (me // (1 << bit)) % 2
    return mine, {"tok": me + (1 - 2 * mine) * (1 << bit)}


def greet(bits):
    barrier = pltpu.get_barrier_semaphore()
    for bit in bits:
        pl.semaphore_signal(barrier, inc=1, device_id=toward(bit)[1], device_id_type=MESH)
    pl.semaphore_wait(barrier, len(bits))


def send(src, dst, send_sem, recv_sem, bit):
    copy = pltpu.make_async_remote_copy(
        src_ref=src, dst_ref=dst, send_sem=send_sem, recv_sem=recv_sem,
        device_id=toward(bit)[1], device_id_type=MESH,
    )
    copy.start()
    return copy


def fetch_kernel(
    levels, choice_ref, tok_ref, arrived_ref, theirs_ref,
    chosen, landed, wanted, choice_send, choice_recv, tok_send, tok_recv,
):
    samples, rows, width = tok_ref.shape
    first = levels - SECTIONS
    greet([first + s for s in range(SECTIONS)])
    asks = [
        send(choice_ref.at[s], wanted.at[s], choice_send.at[s], choice_recv.at[s], first + s)
        for s in range(SECTIONS)
    ]
    copies = []
    for s in reversed(range(SECTIONS)):
        asks[s].wait()
        pick = jnp.broadcast_to(wanted[s, 0:1, 0:1], (SUB, width))
        for i in range(samples):
            value = tok_ref[i, :SUB, :].astype(F32)
            for block in range(1, rows // SUB):
                other = tok_ref[i, block * SUB : (block + 1) * SUB, :].astype(F32)
                value = jnp.where(pick == block, other, value)
            chosen[s, i] = value.astype(BF16)
        copies.append(
            (s, send(chosen.at[s], landed.at[s], tok_send.at[s], tok_recv.at[s], first + s))
        )
    theirs_ref[...] = wanted[...]
    for s, copy in reversed(copies):
        copy.wait()
        arrived_ref[s] = landed[s]


def fetch(levels, choice, tokens):
    samples, _, width = tokens.shape
    vmem = pl.BlockSpec(memory_space=pltpu.VMEM)
    size = (SECTIONS, samples, SUB, width)
    sems = pltpu.SemaphoreType.DMA((SECTIONS,))
    return pl.pallas_call(
        functools.partial(fetch_kernel, levels),
        in_specs=[vmem, vmem],
        out_specs=[vmem, vmem],
        out_shape=[
            jax.ShapeDtypeStruct(size, BF16),
            jax.ShapeDtypeStruct(choice.shape, jnp.int32),
        ],
        scratch_shapes=[
            pltpu.VMEM(size, BF16),
            pltpu.VMEM(size, BF16),
            pltpu.VMEM(choice.shape, jnp.int32),
            sems, sems, sems, sems,
        ],
        compiler_params=pltpu.CompilerParams(collective_id=0, has_side_effects=True),
        name="fetch",
    )(choice, tokens)


def settle_kernel(
    levels, part_ref, gw_ref, go_ref, ret_ref, sum_ref,
    landed, acc, got, full, part_send, part_recv, rs_send, rs_recv, ag_send, ag_recv,
):
    width = go_ref.shape[0]
    for i in range(3):
        acc[i * width : (i + 1) * width, :] = gw_ref[i]
    acc[3 * width :, :] = go_ref[...]
    greet(list(range(levels)))
    half_rows = 2 * width
    straight = list(range(levels))
    orders = (straight, [0] + straight[2:] + [1])
    base = [lane * half_rows for lane in range(2)]
    size, inbox = half_rows, [lane * half_rows for lane in range(2)]
    lanes = range(2)

    def window(ref, start, count):
        return ref.at[pl.ds(pl.multiple_of(start, count), count), :]

    def scatter(lane, step, size):
        bit, half = orders[lane][step], size // 2
        mine, _ = toward(bit)
        away = base[lane] + (1 - mine) * half
        copy = send(
            window(acc, away, half), window(got, inbox[lane], half),
            rs_send.at[lane, step], rs_recv.at[lane, step], bit,
        )
        base[lane] = base[lane] + mine * half
        return copy

    flying = [scatter(lane, 0, size) for lane in lanes]
    first = levels - SECTIONS
    returns = [
        send(part_ref.at[s], landed.at[s], part_send.at[s], part_recv.at[s], first + s)
        for s in reversed(range(SECTIONS))
    ]
    for step in range(levels):
        half = size // 2
        for lane in lanes:
            flying[lane].wait()
            here = pl.ds(pl.multiple_of(base[lane], half), half)
            total = acc[here, :].astype(F32) + got[inbox[lane] : inbox[lane] + half, :].astype(F32)
            inbox[lane] += half
            if step < levels - 1:
                acc[here, :] = total.astype(BF16)
                flying[lane] = scatter(lane, step + 1, half)
            else:
                full[here, :] = total.astype(BF16)
        size = half
    for step in reversed(range(levels)):
        for lane in lanes:
            if step < levels - 1:
                flying[lane].wait()
                base[lane] = base[lane] - toward(orders[lane][step + 1])[0] * (size // 2)
            held = window(full, base[lane], size)
            flying[lane] = send(
                held, held, ag_send.at[lane, step], ag_recv.at[lane, step], orders[lane][step]
            )
        size *= 2
    for lane in lanes:
        flying[lane].wait()
    sum_ref[...] = full[...]
    for copy in returns:
        copy.wait()
    ret_ref[...] = landed[...]


def settle(levels, part, gw, go):
    width = go.shape[0]
    vmem = pl.BlockSpec(memory_space=pltpu.VMEM)
    stack = (4 * width, width)
    four = pltpu.SemaphoreType.DMA((SECTIONS,))
    steps = pltpu.SemaphoreType.DMA((2, levels))
    return pl.pallas_call(
        functools.partial(settle_kernel, levels),
        in_specs=[vmem] * 3,
        out_specs=[vmem] * 2,
        out_shape=[
            jax.ShapeDtypeStruct(part.shape, BF16),
            jax.ShapeDtypeStruct(stack, BF16),
        ],
        scratch_shapes=[pltpu.VMEM(part.shape, BF16)]
        + [pltpu.VMEM(stack, BF16)] * 3
        + [four, four, steps, steps, steps, steps],
        compiler_params=pltpu.CompilerParams(
            collective_id=1, has_side_effects=True
        ),
        name="settle",
    )(part, gw, go)


def finish_kernel(
    start_ref, own_ref, early_ref, late_ref, ctx_ref, dq_ref, wq_ref, wk_ref, wv_ref, wo_ref, sum_ref,
    out_ref, gtok_ref, gq_ref, gk_ref, gv_ref, go_ref, key_grads,
):
    out_ref[0] = mm(ctx_ref[0], wo_ref[...]).astype(BF16)
    key_grads[...] = own_ref[:, 0]
    for s in range(SECTIONS):
        at = pl.ds(pl.multiple_of(start_ref[s], SUB), SUB)
        cut = early_ref.shape[-1]
        key_grads[:, at, :cut] += early_ref[s, :, 0].astype(F32)
        key_grads[:, at, cut:] += late_ref[s, :, 0].astype(F32)
    gtok_ref[0] = (
        nt(dq_ref[0], wq_ref[...])
        + nt(key_grads[0].astype(BF16), wk_ref[...])
        + nt(key_grads[1].astype(BF16), wv_ref[...])
    ).astype(BF16)
    for i, ref in enumerate((gq_ref, gk_ref, gv_ref, go_ref)):
        ref[...] = sum_ref[i].astype(F32)


def finish(starts, own, early, late, ctx, dq, w_query, w_key, w_value, w_out, sums):
    samples, rows, width = ctx.shape
    row = pl.BlockSpec((1, rows, width), lambda i: (i, 0, 0))
    weight = pl.BlockSpec((width, width), lambda i: (0, 0))
    share = width // samples
    grad = pl.BlockSpec((share, width), lambda i: (i, 0))
    return pl.pallas_call(
        finish_kernel,
        grid=(samples,),
        in_specs=[
            pl.BlockSpec(memory_space=pltpu.SMEM),
            pl.BlockSpec((2, 1, rows, width), lambda i: (0, i, 0, 0)),
            pl.BlockSpec((SECTIONS, 2, 1, SUB, early.shape[-1]), lambda i: (0, 0, i, 0, 0)),
            pl.BlockSpec((SECTIONS, 2, 1, SUB, late.shape[-1]), lambda i: (0, 0, i, 0, 0)),
            row, row, weight, weight, weight, weight,
            pl.BlockSpec((4, share, width), lambda i: (0, i, 0)),
        ],
        out_specs=[row, row, grad, grad, grad, grad],
        out_shape=[jax.ShapeDtypeStruct(ctx.shape, BF16)] * 2
        + [jax.ShapeDtypeStruct((width, width), F32)] * 4,
        scratch_shapes=[pltpu.VMEM((2, rows, width), F32)],
        name="finish",
    )(starts, own, early, late, ctx, dq, w_query, w_key, w_value, w_out, sums)


def per_device(tokens, w_query, w_key, w_value, w_out, partner_block, head_masks, cotangent):
    width = tokens.shape[2]
    levels = lax.axis_size("tok").bit_length() - 1
    head_width = width // head_masks.shape[2]
    choice = jnp.broadcast_to(partner_block[0][:, None, None], (SECTIONS, 8, LANES))
    arrived, theirs = fetch(levels, choice, tokens)
    groups = width // LANES
    inputs = (head_masks, tokens, arrived, cotangent, w_query, w_key, w_value, w_out)
    *held, part = attend(head_width, 0, groups - LATE, (), *inputs)
    early = []
    for s in range(SECTIONS):
        early.append(partner(part[s], "tok", levels - SECTIONS + s))
    ctx, dq, own, gw, go, part = attend(head_width, groups - LATE, LATE, tuple(held), *inputs)
    late, sums = settle(levels, part, gw, go)
    starts = theirs[:, 0, 0] * SUB
    return finish(
        starts, own, jnp.stack(early), late, ctx, dq, w_query, w_key, w_value, w_out,
        sums.reshape(4, width, width),
    )


def solution(mesh):
    placed = (
        P("groups", "tok", None),
        P(),
        P(),
        P(),
        P(),
        P("tok", None),
        P("tok", None, None),
        P("groups", "tok", None),
    )
    return jax.shard_map(
        per_device,
        mesh=mesh,
        in_specs=placed,
        out_specs=(
            P("groups", "tok", None),
            P("groups", "tok", None),
            P("groups", None),
            P("groups", None),
            P("groups", None),
            P("groups", None),
        ),
        check_vma=False,
    )
```
